256 devices in a mesh: modes: 8 (over z_hi, x), space: 32 (over z_lo, y, core).
Axes of the slice: x: 4, y: 4, z: 8 (z_hi: 2, z_lo: 4; z = z_hi * 4 + z_lo), core: 2. Of those that a mesh axis runs over, the one named last changes fastest.
Arguments:
- mode_coeffs: float32 [120, 32, 120, 128], P('modes', 'space'), may hold values from -6 to 6
- mean_perm: float32 [32, 120, 128], P('space'), may hold values from 0.5 to 2
- kl_fields: float32 [7, 32, 120, 128], P(None, 'space'), may hold values from -4 to 4
- couplings: float32 [7, 120, 120], replicated, may hold values from -0.5 to 0.5
Outputs:
- applied: float32 [120, 32, 120, 128], P('modes', 'space')
The draws below stay inside these ranges and needn't reach their ends.
All inputs are finite; a program needn't handle non-finite values.
Results may differ from the reference program's by a relative error of at most 0.0001.
Values sent between devices are 32-bit elements; how exact they have to be, the bound alone decides.
A program may use at most 192 MiB of HBM per device.

```python
import math
import jax
import jax.numpy as jnp
from jax import lax

MODES = 120
KL = 7
NY = 120
NZ = 128
NX = 32


def level_of(stream_key, dims, cuts, low, high):
    loudness, own = 1.0, jax.random.fold_in(stream_key, 6)
    for axis_at, blocks in cuts:
        heights = jnp.exp(jax.random.uniform(jax.random.fold_in(own, axis_at), (blocks,), jnp.float32, low / len(cuts), high / len(cuts)))
        loudness = loudness * jnp.repeat(heights, dims[axis_at] // blocks).reshape([-1 if axis == axis_at else 1 for axis in range(len(dims))])
    return loudness


def normal_values(own_key, dims, scale, bound, cuts=(), kind=jnp.bfloat16):
    factor_of = level_of(own_key, dims, cuts, -0.22, 0.18) if cuts else 1.0
    values = jax.random.normal(own_key, dims, jnp.float32) * scale * factor_of
    return jnp.minimum(jnp.maximum(values, -bound), bound).astype(kind)


def setup_inputs(seed: int = 0) -> dict:
    seeds = jax.random.split(jax.random.key(seed), 5)
    return {
        "mode_coeffs": normal_values(seeds[0], (MODES, NX, NY, NZ), 1.0, 6.0, ((0, 8), (1, 32)), jnp.float32),
        "mean_perm": jnp.clip(jnp.exp(math.log(2.0) - 1.3862944 * jax.random.uniform(seeds[1], (NX, NY, NZ), jnp.float32) ** level_of(seeds[1], (NX, NY, NZ), ((0, 32),), -0.2, 0.2)), 0.5, 2.0),
        "kl_fields": normal_values(seeds[2], (KL, NX, NY, NZ), 0.3, 4.0, ((1, 32),), jnp.float32),
        "couplings": normal_values(seeds[3], (KL, MODES, MODES), MODES ** -0.5, 0.5, (), jnp.float32),
    }


def shifted(padded, direction, offset):
    result = padded
    base = padded.ndim - 3
    for axis_index in range(3):
        extent = padded.shape[base + axis_index] - 2
        begin = offset if axis_index == direction else 1
        result = lax.slice_in_dim(result, begin, begin + extent, axis=base + axis_index)
    return result


def operate(field_pad, perm_pad):
    centre = shifted(field_pad, 0, 1)
    centre_perm = shifted(perm_pad, 0, 1)
    terms = []
    for direction in range(3):
        for offset in (0, 2):
            face_perm = 0.5 * (centre_perm + shifted(perm_pad, direction, offset))
            terms.append(face_perm * (centre - shifted(field_pad, direction, offset)))
    accum_total = terms[0]
    for extra_term in terms[1:]:
        accum_total = accum_total + extra_term
    return accum_total


def pad_cells(source):
    widths = [(0, 0)] * (source.ndim - 3) + [(1, 1)] * 3
    return jnp.pad(source, widths)


def reference(mode_coeffs, mean_perm, kl_fields, couplings):
    flat_modes = mode_coeffs.reshape(mode_coeffs.shape[0], -1)
    result = operate(pad_cells(mode_coeffs), pad_cells(mean_perm))
    for term_index in range(KL):
        mixed_modes = jnp.dot(couplings[term_index], flat_modes, precision=lax.Precision.HIGHEST).reshape(mode_coeffs.shape)
        result = result + operate(pad_cells(mixed_modes), pad_cells(kl_fields[term_index]))
    return result
```

```python
import functools

import jax
import jax.numpy as jnp
from jax import lax
from jax.experimental import pallas as pl
from jax.experimental.pallas import tpu as pltpu
from jax.sharding import PartitionSpec as P

MESH = pl.DeviceIdType.MESH
F32, BF16 = jnp.float32, jnp.bfloat16

MD = 15
MP = 16
NX = 4
NY, NZ = 120, 128
KT = 8
R = 8
NC = NY // R
AHEAD = 3
OUT2 = 2 * MP
PR = NY + 16
KD = 3 * NX * MP


def kernel(u, mean, kl, cpl, out, gath, fld, flo, fhi, cplv, cf, w, part, tlo, thi, hlo, hhi, zr,
           carry, sem_l, sx_s, sx_r, sf_s, sh_s, sh_r, sz_s, sz_r, ff_s, ff_r):
    m = lax.axis_index("modes")
    s = lax.axis_index("space")
    x = lax.rem(m, NX)
    zhi = m // NX
    first, last = s == 0, s == 31
    xr = zhi * NX + lax.rem(x + 1, NX)
    xl = zhi * NX + lax.rem(x + NX - 1, NX)
    zp = lax.rem(m + NX, 2 * NX)

    barrier = pltpu.get_barrier_semaphore()

    def greet(dev):
        pl.semaphore_signal(barrier, inc=1, device_id=dev, device_id_type=MESH)

    greet((xr, s))
    greet((xl, s))
    greet((zp, s))

    @pl.when(jnp.logical_not(first))
    def _():
        greet((m, s - 1))

    @pl.when(jnp.logical_not(last))
    def _():
        greet((m, s + 1))

    local = [
        pltpu.make_async_copy(u, gath.at[x, 0:MD], sem_l.at[0]),
        pltpu.make_async_copy(mean, fld.at[0], sem_l.at[1]),
        pltpu.make_async_copy(kl, fld.at[1:KT], sem_l.at[2]),
        pltpu.make_async_copy(cpl, cplv, sem_l.at[3]),
    ]
    for copy in local:
        copy.start()

    gath[:, MD] = jnp.zeros((NX, NY, NZ), F32)

    @pl.when(first)
    def _():
        flo[...] = jnp.zeros(flo.shape, F32)
        hlo[...] = jnp.zeros(hlo.shape, F32)

    @pl.when(last)
    def _():
        fhi[...] = jnp.zeros(fhi.shape, F32)
        hhi[...] = jnp.zeros(hhi.shape, F32)

    carry[...] = jnp.zeros(carry.shape, F32)

    pl.semaphore_wait(barrier, 5 - first.astype(jnp.int32) - last.astype(jnp.int32))

    def remote(src, dst, send, recv, dev):
        return pltpu.make_async_remote_copy(
            src_ref=src, dst_ref=dst, send_sem=send, recv_sem=recv, device_id=dev, device_id_type=MESH
        )

    def rows(c, base=0):
        return pl.ds(pl.multiple_of(base + c * R, R), R)

    def own_right(c):
        return remote(u.at[:, rows(c)], gath.at[x, 0:MD, rows(c)], sx_s.at[0, c], sx_r.at[0, c], (xr, s))

    def own_left(c):
        return remote(u.at[:, rows(c)], gath.at[x, 0:MD, rows(c)], sx_s.at[1, c], sx_r.at[1, c], (xl, s))

    x_l, x_r = lax.rem(x + NX - 1, NX), lax.rem(x + 1, NX)

    def got_left(c):
        return remote(u.at[:, rows(c)], gath.at[x_l, 0:MD, rows(c)], sx_s.at[0, c], sx_r.at[0, c], (xr, s))

    def got_right(c):
        return remote(u.at[:, rows(c)], gath.at[x_r, 0:MD, rows(c)], sx_s.at[1, c], sx_r.at[1, c], (xl, s))

    def on_right(c):
        ref = gath.at[x_l, 0:MD, rows(c)]
        return remote(ref, ref, sf_s.at[c], sx_r.at[2, c], (xr, s))

    def on_left(c):
        ref = gath.at[x_r, 0:MD, rows(c)]
        return remote(ref, ref, sf_s.at[c], sx_r.at[2, c], (xl, s))

    def got_far(c):
        ref = gath.at[lax.rem(x + 2, NX), 0:MD, rows(c)]
        return remote(ref, ref, sf_s.at[c], sx_r.at[2, c], (xr, s))

    def fields(i, dev, dst):
        return [
            remote(mean, dst.at[0], ff_s.at[i, 0], ff_r.at[i, 0], dev),
            remote(kl, dst.at[1:KT], ff_s.at[i, 1], ff_r.at[i, 1], dev),
        ]

    up_f = fields(0, (m, s + 1), flo)
    down_f = fields(1, (m, s - 1), fhi)

    def halo_up(c):
        return remote(thi.at[:, 0:MD, rows(c)], hlo.at[:, 0:MD, rows(c)], sh_s.at[0, c], sh_r.at[0, c], (m, s + 1))

    def halo_down(c):
        return remote(tlo.at[:, 0:MD, rows(c)], hhi.at[:, 0:MD, rows(c)], sh_s.at[1, c], sh_r.at[1, c], (m, s - 1))

    def across(c):
        return remote(part.at[1, 0:MD, rows(c, R)], zr.at[:, rows(c)], sz_s.at[c], sz_r.at[c], (zp, s))

    @pl.when(jnp.logical_not(last))
    def _():
        for copy in up_f:
            copy.start()

    @pl.when(jnp.logical_not(first))
    def _():
        for copy in down_f:
            copy.start()

    for c in range(AHEAD):
        own_right(c).start()
        own_left(c).start()

    local[3].wait()
    ri = lax.broadcasted_iota(jnp.int32, (OUT2, NY), 0)
    rc = lax.broadcasted_iota(jnp.int32, (OUT2, NY), 1)
    ro, rm = ri // MP, lax.rem(ri, MP)
    row_of = jnp.where(ro == 0, m, zp) * MD + rm
    pick = jnp.where((rc == row_of) & (rm < MD), 1.0, 0.0).astype(BF16)
    ci = lax.broadcasted_iota(jnp.int32, (NY, KD), 0)
    cj = lax.broadcasted_iota(jnp.int32, (NY, KD), 1)
    blk, cs = cj // (NX * MP), lax.rem(cj, NX * MP)
    cm = lax.rem(cs, MP)
    hit = (ci == zhi * (NX * MD) + (cs // MP) * MD + cm) & (cm < MD)
    put_hi = jnp.where(hit & (blk < 2), 1.0, 0.0).astype(BF16)
    put_lo = jnp.where(hit & (blk == 2), 1.0, 0.0).astype(BF16)
    di = lax.broadcasted_iota(jnp.int32, (OUT2, KD), 0)
    dj = lax.broadcasted_iota(jnp.int32, (OUT2, KD), 1)
    same = (di < MD) & (dj < 2 * NX * MP) & (lax.rem(dj, NX * MP) == x * MP + di)
    w[0:OUT2] = jnp.where(same, 1.0, 0.0).astype(BF16)

    def dot(a, b):
        return jnp.dot(a, b, preferred_element_type=F32)

    for k in range(1, KT):
        full = cplv[k - 1]
        hi = full.astype(BF16)
        lo = (full - hi.astype(F32)).astype(BF16)
        rows_hi = dot(pick, hi).astype(BF16)
        rows_lo = dot(pick, lo).astype(BF16)
        w[k * OUT2:(k + 1) * OUT2] = (dot(rows_hi, put_hi) + dot(rows_lo, put_lo)).astype(BF16)

    local[1].wait()
    local[2].wait()
    lane = lax.broadcasted_iota(jnp.int32, (NY, NZ), 1)
    none = jnp.zeros((1, NZ), F32)
    for k in range(KT):
        a = fld[k]
        cf[2, k, 0:NY + 1] = 0.5 * (jnp.concatenate([none, a], 0) + jnp.concatenate([a, none], 0))
        cf[3, k, 0:NY] = 0.5 * (a + jnp.where(lane == 0, 0.0, pltpu.roll(a, 1, 1)))
        cf[4, k, 0:NY] = 0.5 * (a + jnp.where(lane == NZ - 1, 0.0, pltpu.roll(a, NZ - 1, 1)))

    @pl.when(jnp.logical_not(first))
    def _():
        for copy in up_f:
            copy.wait_recv()

    @pl.when(jnp.logical_not(last))
    def _():
        for copy in down_f:
            copy.wait_recv()

    for k in range(KT):
        cf[0, k, 0:NY] = 0.5 * (fld[k] + flo[k])
        cf[1, k, 0:NY] = 0.5 * (fld[k] + fhi[k])

    local[0].wait()

    gflat = gath.reshape(NX * MP * NY, NZ)
    pflat = part.reshape(OUT2 * PR, NZ)
    tlo_flat = tlo.reshape(OUT2 * NY, NZ)
    thi_flat = thi.reshape(OUT2 * NY, NZ)
    lane2 = lax.broadcasted_iota(jnp.int32, (OUT2, NZ), 1)

    def compute(c):
        def pair(q, held):
            acc, above = held
            r0 = c * R + 2 * q
            cols = []
            for a in range(2):
                xf = gflat[pl.ds(r0 + a, NX * MP, stride=NY), :]
                hi = xf.astype(BF16)
                lo = (xf - hi.astype(F32)).astype(BF16)
                cols.append(jnp.concatenate([hi, lo, hi], 0))
            v = dot(w[...], jnp.concatenate(cols, 1))
            for a in range(2):
                r = r0 + a
                sums = [None] * 6
                for k in range(KT):
                    vk = v[k * OUT2:(k + 1) * OUT2, a * NZ:(a + 1) * NZ]
                    for d, (kind, at) in enumerate(((0, 0), (1, 0), (2, 0), (2, 1), (3, 0), (4, 0))):
                        term = cf[kind, k, pl.ds(r + at, 1), :] * vk
                        sums[d] = term if sums[d] is None else sums[d] + term
                xlo, xhi, ylo, yhi, zlo, zhi_ = sums
                tlo_flat[pl.ds(r, OUT2, stride=NY), :] = xlo
                thi_flat[pl.ds(r, OUT2, stride=NY), :] = xhi
                pflat[pl.ds(r + R - 1, OUT2, stride=PR), :] = acc - ylo
                acc = ((xlo + xhi) + (ylo + yhi)) + (zlo + zhi_) - above
                acc = acc - jnp.where(lane2 == 0, 0.0, pltpu.roll(zhi_, 1, 1))
                acc = acc - jnp.where(lane2 == NZ - 1, 0.0, pltpu.roll(zlo, NZ - 1, 1))
                above = yhi
            return acc, above

        acc, above = lax.fori_loop(0, R // 2, pair, (carry[0], carry[1]))
        carry[0] = acc
        carry[1] = above

    def step(t, _):
        @pl.when(t + AHEAD < NC)
        def _():
            own_right(t + AHEAD).start()
            own_left(t + AHEAD).start()

        @pl.when(t < NC)
        def _():
            got_left(t).wait_recv()
            got_right(t).wait_recv()

            @pl.when(lax.rem(t, 2) == 0)
            def _():
                on_right(t).start()

            @pl.when(lax.rem(t, 2) == 1)
            def _():
                on_left(t).start()

        @pl.when((t >= 1) & (t < NC + 1))
        def _():
            c = t - 1
            got_far(c).wait_recv()
            compute(c)

            @pl.when(jnp.logical_not(last))
            def _():
                halo_up(c).start()

            @pl.when(jnp.logical_not(first))
            def _():
                halo_down(c).start()

            @pl.when(c == NC - 1)
            def _():
                pflat[pl.ds(NY - 1 + R, OUT2, stride=PR), :] = carry[0]

        @pl.when(t >= 2)
        def _():
            c = t - 2

            @pl.when(jnp.logical_not(first))
            def _():
                halo_up(c).wait_recv()

            @pl.when(jnp.logical_not(last))
            def _():
                halo_down(c).wait_recv()

            part[:, 0:MD, rows(c, R)] = part[:, 0:MD, rows(c, R)] - (hlo[:, 0:MD, rows(c)] + hhi[:, 0:MD, rows(c)])
            across(c).start()

        return 0

    lax.fori_loop(0, NC + 2, step, 0)

    def finish(c, _):
        across(c).wait_recv()
        out[:, rows(c)] = part[0, 0:MD, rows(c, R)] + zr[:, rows(c)]
        return 0

    lax.fori_loop(0, NC, finish, 0)

    def drain(c, _):
        own_right(c).wait_send()
        own_left(c).wait_send()
        on_right(c).wait_send()
        across(c).wait_send()

        @pl.when(jnp.logical_not(last))
        def _():
            halo_up(c).wait_send()

        @pl.when(jnp.logical_not(first))
        def _():
            halo_down(c).wait_send()

        return 0

    lax.fori_loop(0, NC, drain, 0)

    @pl.when(jnp.logical_not(last))
    def _():
        for copy in up_f:
            copy.wait_send()

    @pl.when(jnp.logical_not(first))
    def _():
        for copy in down_f:
            copy.wait_send()


def local(mode_coeffs, mean_perm, kl_fields, couplings):
    dma = pltpu.SemaphoreType.DMA
    hbm = pl.BlockSpec(memory_space=pl.ANY)
    vmem = pltpu.VMEM
    res = pl.pallas_call(
        kernel,
        out_shape=jax.ShapeDtypeStruct((MD, NY, NZ), F32),
        in_specs=[hbm] * 4,
        out_specs=pl.BlockSpec(memory_space=pltpu.VMEM),
        scratch_shapes=[
            vmem((NX, MP, NY, NZ), F32),
            vmem((KT, NY, NZ), F32),
            vmem((KT, NY, NZ), F32),
            vmem((KT, NY, NZ), F32),
            vmem((KT - 1, NY, NY), F32),
            vmem((5, KT, 128, NZ), F32),
            vmem((KT * OUT2, KD), BF16),
            vmem((2, MP, PR, NZ), F32),
            vmem((2, MP, NY, NZ), F32),
            vmem((2, MP, NY, NZ), F32),
            vmem((2, MP, NY, NZ), F32),
            vmem((2, MP, NY, NZ), F32),
            vmem((MD, NY, NZ), F32),
            vmem((2, OUT2, NZ), F32),
            dma((4,)),
            dma((2, NC)), dma((3, NC)), dma((NC,)),
            dma((2, NC)), dma((2, NC)),
            dma((NC,)), dma((NC,)),
            dma((2, 2)), dma((2, 2)),
        ],
        compiler_params=pltpu.CompilerParams(
            collective_id=0, has_side_effects=True, vmem_limit_bytes=56 * 1024 * 1024
        ),
    )(mode_coeffs.reshape(MD, NY, NZ), mean_perm.reshape(NY, NZ), kl_fields.reshape(KT - 1, NY, NZ), couplings)
    return res.reshape(MD, 1, NY, NZ)


def solution(mesh):
    in_specs = (
        P("modes", "space", None, None),
        P("space", None, None),
        P(None, "space", None, None),
        P(),
    )
    out_specs = P("modes", "space", None, None)
    return jax.shard_map(local, mesh=mesh, in_specs=in_specs, out_specs=out_specs, check_vma=False)
```

```python
import functools

import jax
import jax.numpy as jnp
from jax import lax
from jax.experimental import pallas as pl
from jax.experimental.pallas import tpu as pltpu
from jax.sharding import PartitionSpec as P

MESH = pl.DeviceIdType.MESH
F32, BF16 = jnp.float32, jnp.bfloat16

MD = 15
MP = 16
NX = 4
NY, NZ = 120, 128
KT = 8
R = 8
NC = NY // R
LINE = 8
OUT2 = 2 * MP
PR = NY + 16
KD = 3 * NX * MP
LAG = 4


def kernel(u, mean, kl, cpl, out, zr, gath, fld, flo, fhi, rfl, cplv, cf, w, part, tlo, thi, hlo, hhi, rel,
           carry, sem_l, sem_o, sx_s, sx_r, sh_s, sh_r, sr_s, sr_r, sz_s, sz_r, ff_s, ff_r, fr_s, fr_r):
    m = lax.axis_index("modes")
    s = lax.axis_index("space")
    x = lax.rem(m, NX)
    zhi = m // NX
    first, last = s == 0, s == 31
    xr = zhi * NX + lax.rem(x + 1, NX)
    xl = zhi * NX + lax.rem(x + NX - 1, NX)
    zp = lax.rem(m + NX, 2 * NX)

    xf = zhi * NX + lax.rem(x + 2, NX)

    y, core, zlo = lax.rem(s, LINE) // 2, lax.rem(s, 2), s // LINE
    line = zlo * LINE
    up, down = jnp.logical_not(last), jnp.logical_not(first)
    seam_up = (core == 1) & (y == 3) & (zlo < 3)
    seam_down = (core == 0) & (y == 0) & (zlo > 0)
    relay_up = (core == 1) & (y == 0) & (zlo < 3)
    relay_down = (core == 0) & (y == 3) & (zlo > 0)
    seam, relay = seam_up | seam_down, relay_up | relay_down
    goal = jnp.where(core == 1, line + LINE, line - 1)
    origin = jnp.where(core == 1, line + LINE - 1, line)
    aside = jnp.where(core == 1, line + 1, line + LINE - 2)

    barrier = pltpu.get_barrier_semaphore()

    def greet(dev):
        pl.semaphore_signal(barrier, inc=1, device_id=dev, device_id_type=MESH)

    greet((xr, s))
    greet((xl, s))
    greet((xf, s))
    greet((zp, s))

    @pl.when(down)
    def _():
        greet((m, s - 1))

    @pl.when(up)
    def _():
        greet((m, s + 1))

    @pl.when(relay)
    def _():
        greet((m, origin))

    @pl.when(seam_down)
    def _():
        greet((m, line - LINE + 1))
        greet((m, aside))

    @pl.when(seam_up)
    def _():
        greet((m, line + LINE + LINE - 2))
        greet((m, aside))

    local = [
        pltpu.make_async_copy(u, gath.at[x, 0:MD], sem_l.at[0]),
        pltpu.make_async_copy(mean, fld.at[0], sem_l.at[1]),
        pltpu.make_async_copy(kl, fld.at[1:KT], sem_l.at[2]),
        pltpu.make_async_copy(cpl, cplv, sem_l.at[3]),
    ]
    for copy in local:
        copy.start()

    gath[:, MD] = jnp.zeros((NX, NY, NZ), F32)

    @pl.when(first)
    def _():
        flo[...] = jnp.zeros(flo.shape, F32)
        hlo[...] = jnp.zeros(hlo.shape, F32)

    @pl.when(last)
    def _():
        fhi[...] = jnp.zeros(fhi.shape, F32)
        hhi[...] = jnp.zeros(hhi.shape, F32)

    carry[...] = jnp.zeros(carry.shape, F32)

    one = jnp.int32
    pl.semaphore_wait(barrier, 4 + up.astype(one) + down.astype(one) + 2 * relay.astype(one) + seam.astype(one))

    def remote(src, dst, send, recv, dev):
        return pltpu.make_async_remote_copy(
            src_ref=src, dst_ref=dst, send_sem=send, recv_sem=recv, device_id=dev, device_id_type=MESH
        )

    def rows(c, base=0):
        return pl.ds(pl.multiple_of(base + c * R, R), R)

    x_from = [lax.rem(x + NX - 1, NX), lax.rem(x + 1, NX), lax.rem(x + 2, NX)]
    x_to = [xr, xl, xf]

    def own(i, c):
        return remote(u.at[:, rows(c)], gath.at[x, 0:MD, rows(c)], sx_s.at[i, c], sx_r.at[i, c], (x_to[i], s))

    def got(i, c):
        ref = gath.at[x_from[i], 0:MD, rows(c)]
        return remote(ref, ref, sx_s.at[i, c], sx_r.at[i, c], (x_to[i], s))

    def field(k):
        return mean if k == 0 else kl.at[k - 1]

    def field_up(k):
        return remote(field(k), flo.at[k], ff_s.at[0, k], ff_r.at[0, k], (m, s + 1))

    def field_down(k):
        return remote(field(k), fhi.at[k], ff_s.at[1, k], ff_r.at[1, k], (m, s - 1))

    def field_aside(k):
        return remote(field(k), rfl.at[k], ff_s.at[core ^ 1, k], fr_r.at[k], (m, aside))

    def field_relay_up(k):
        return remote(rfl.at[k], flo.at[k], fr_s.at[k], ff_r.at[0, k], (m, goal))

    def field_relay_down(k):
        return remote(rfl.at[k], fhi.at[k], fr_s.at[k], ff_r.at[1, k], (m, goal))

    def halo_up(c):
        return remote(thi.at[:, 0:MD, rows(c)], hlo.at[:, 0:MD, rows(c)], sh_s.at[0, c], sh_r.at[0, c], (m, s + 1))

    def halo_down(c):
        return remote(tlo.at[:, 0:MD, rows(c)], hhi.at[:, 0:MD, rows(c)], sh_s.at[1, c], sh_r.at[1, c], (m, s - 1))

    def aside_up(c):
        return remote(thi.at[:, 0:MD, rows(c)], rel.at[:, 0:MD, rows(c)], sh_s.at[0, c], sr_r.at[c],
                      (m, aside))

    def aside_down(c):
        return remote(tlo.at[:, 0:MD, rows(c)], rel.at[:, 0:MD, rows(c)], sh_s.at[1, c], sr_r.at[c],
                      (m, aside))

    def relay_on_up(c):
        return remote(rel.at[:, 0:MD, rows(c)], hlo.at[:, 0:MD, rows(c)], sr_s.at[c], sh_r.at[0, c], (m, goal))

    def relay_on_down(c):
        return remote(rel.at[:, 0:MD, rows(c)], hhi.at[:, 0:MD, rows(c)], sr_s.at[c], sh_r.at[1, c], (m, goal))

    def across(c):
        return remote(part.at[1, 0:MD, rows(c, R)], zr.at[:, rows(c)], sz_s.at[c], sz_r.at[c], (zp, s))

    def keep(c):
        return pltpu.make_async_copy(part.at[0, 0:MD, rows(c, R)], out.at[:, rows(c)], sem_o.at[c])

    def when(cond, fn):
        pl.when(cond)(fn)

    for k in range(KT):
        direct_up, direct_down = up, down
        if k % 2 == 0:
            direct_up, direct_down = up & jnp.logical_not(seam_up), down & jnp.logical_not(seam_down)
            when(seam, lambda: field_aside(k).start())
        when(direct_up, lambda: field_up(k).start())
        when(direct_down, lambda: field_down(k).start())

    def gather(c, _):
        for i in range(3):
            own(i, c).start()
        return 0

    lax.fori_loop(0, NC, gather, 0)

    local[3].wait()
    ri = lax.broadcasted_iota(jnp.int32, (OUT2, NY), 0)
    rc = lax.broadcasted_iota(jnp.int32, (OUT2, NY), 1)
    ro, rm = ri // MP, lax.rem(ri, MP)
    row_of = jnp.where(ro == 0, m, zp) * MD + rm
    pick = jnp.where((rc == row_of) & (rm < MD), 1.0, 0.0).astype(BF16)
    ci = lax.broadcasted_iota(jnp.int32, (NY, KD), 0)
    cj = lax.broadcasted_iota(jnp.int32, (NY, KD), 1)
    blk, cs = cj // (NX * MP), lax.rem(cj, NX * MP)
    cm = lax.rem(cs, MP)
    hit = (ci == zhi * (NX * MD) + (cs // MP) * MD + cm) & (cm < MD)
    put_hi = jnp.where(hit & (blk < 2), 1.0, 0.0).astype(BF16)
    put_lo = jnp.where(hit & (blk == 2), 1.0, 0.0).astype(BF16)
    di = lax.broadcasted_iota(jnp.int32, (OUT2, KD), 0)
    dj = lax.broadcasted_iota(jnp.int32, (OUT2, KD), 1)
    same = (di < MD) & (dj < 2 * NX * MP) & (lax.rem(dj, NX * MP) == x * MP + di)
    w[0:OUT2] = jnp.where(same, 1.0, 0.0).astype(BF16)

    def dot(a, b):
        return jnp.dot(a, b, preferred_element_type=F32)

    for k in range(1, KT):
        full = cplv[k - 1]
        hi = full.astype(BF16)
        lo = (full - hi.astype(F32)).astype(BF16)
        rows_hi = dot(pick, hi).astype(BF16)
        rows_lo = dot(pick, lo).astype(BF16)
        w[k * OUT2:(k + 1) * OUT2] = (dot(rows_hi, put_hi) + dot(rows_lo, put_lo)).astype(BF16)

    local[1].wait()
    local[2].wait()
    lane = lax.broadcasted_iota(jnp.int32, (NY, NZ), 1)
    none = jnp.zeros((1, NZ), F32)
    for k in range(KT):
        a = fld[k]
        cf[2, k, 0:NY + 1] = 0.5 * (jnp.concatenate([none, a], 0) + jnp.concatenate([a, none], 0))
        cf[3, k, 0:NY] = 0.5 * (a + jnp.where(lane == 0, 0.0, pltpu.roll(a, 1, 1)))
        cf[4, k, 0:NY] = 0.5 * (a + jnp.where(lane == NZ - 1, 0.0, pltpu.roll(a, NZ - 1, 1)))

    for k in range(0, KT, 2):
        @pl.when(relay)
        def _():
            field_aside(k).wait_recv()
            when(core == 1, lambda: field_relay_up(k).start())
            when(core == 0, lambda: field_relay_down(k).start())

    for k in range(KT):
        when(down, lambda: field_up(k).wait_recv())
        when(up, lambda: field_down(k).wait_recv())

    for k in range(KT):
        cf[0, k, 0:NY] = 0.5 * (fld[k] + flo[k])
        cf[1, k, 0:NY] = 0.5 * (fld[k] + fhi[k])

    local[0].wait()

    gflat = gath.reshape(NX * MP * NY, NZ)
    pflat = part.reshape(OUT2 * PR, NZ)
    tlo_flat = tlo.reshape(OUT2 * NY, NZ)
    thi_flat = thi.reshape(OUT2 * NY, NZ)
    lane2 = lax.broadcasted_iota(jnp.int32, (OUT2, NZ), 1)

    def compute(c):
        def pair(q, held):
            acc, above = held
            r0 = c * R + 2 * q
            cols = []
            for a in range(2):
                xf = gflat[pl.ds(r0 + a, NX * MP, stride=NY), :]
                hi = xf.astype(BF16)
                lo = (xf - hi.astype(F32)).astype(BF16)
                cols.append(jnp.concatenate([hi, lo, hi], 0))
            v = dot(w[...], jnp.concatenate(cols, 1))
            for a in range(2):
                r = r0 + a
                sums = [None] * 6
                for k in range(KT):
                    vk = v[k * OUT2:(k + 1) * OUT2, a * NZ:(a + 1) * NZ]
                    for d, (kind, at) in enumerate(((0, 0), (1, 0), (2, 0), (2, 1), (3, 0), (4, 0))):
                        term = cf[kind, k, pl.ds(r + at, 1), :] * vk
                        sums[d] = term if sums[d] is None else sums[d] + term
                xlo, xhi, ylo, yhi, zlo, zhi_ = sums
                tlo_flat[pl.ds(r, OUT2, stride=NY), :] = xlo
                thi_flat[pl.ds(r, OUT2, stride=NY), :] = xhi
                pflat[pl.ds(r + R - 1, OUT2, stride=PR), :] = acc - ylo
                acc = ((xlo + xhi) + (ylo + yhi)) + (zlo + zhi_) - above
                acc = acc - jnp.where(lane2 == 0, 0.0, pltpu.roll(zhi_, 1, 1))
                acc = acc - jnp.where(lane2 == NZ - 1, 0.0, pltpu.roll(zlo, NZ - 1, 1))
                above = yhi
            return acc, above

        acc, above = lax.fori_loop(0, R // 2, pair, (carry[0], carry[1]))
        carry[0] = acc
        carry[1] = above

    def send_halos(c):
        even = lax.rem(c, 2) == 0
        off_up, off_down = seam_up & even, seam_down & even
        when(up & jnp.logical_not(off_up), lambda: halo_up(c).start())
        when(down & jnp.logical_not(off_down), lambda: halo_down(c).start())
        when(off_up, lambda: aside_up(c).start())
        when(off_down, lambda: aside_down(c).start())

    def relays(c):
        return relay & (lax.rem(c, 2) == 0)

    def step(t, _):
        @pl.when(t < NC)
        def _():
            for i in range(3):
                got(i, t).wait_recv()

        @pl.when((t >= 1) & (t <= NC) & relays(t + 1))
        def _():
            c = t - 1
            aside_up(c).wait_recv()
            when(core == 1, lambda: relay_on_up(c).start())
            when(core == 0, lambda: relay_on_down(c).start())

        @pl.when(t < NC)
        def _():
            compute(t)
            send_halos(t)

            @pl.when(t == NC - 1)
            def _():
                pflat[pl.ds(NY - 1 + R, OUT2, stride=PR), :] = carry[0]

        @pl.when(t >= LAG)
        def _():
            c = t - LAG
            when(down, lambda: halo_up(c).wait_recv())
            when(up, lambda: halo_down(c).wait_recv())
            part[:, 0:MD, rows(c, R)] = part[:, 0:MD, rows(c, R)] - (hlo[:, 0:MD, rows(c)] + hhi[:, 0:MD, rows(c)])
            across(c).start()
            keep(c).start()

        return 0

    lax.fori_loop(0, NC + LAG, step, 0)

    def drain(c, _):
        for i in range(3):
            own(i, c).wait_send()
        when(up, lambda: halo_up(c).wait_send())
        when(down, lambda: halo_down(c).wait_send())
        when(relays(c), lambda: relay_on_up(c).wait_send())
        keep(c).wait()
        across(c).wait_send()
        across(c).wait_recv()
        return 0

    for k in range(KT):
        when(up, lambda: field_up(k).wait_send())
        when(down, lambda: field_down(k).wait_send())
        if k % 2 == 0:
            when(relay, lambda: field_relay_up(k).wait_send())

    lax.fori_loop(0, NC, drain, 0)


def local(mode_coeffs, mean_perm, kl_fields, couplings):
    dma = pltpu.SemaphoreType.DMA
    hbm = pl.BlockSpec(memory_space=pl.ANY)
    vmem = pltpu.VMEM
    plane = jax.ShapeDtypeStruct((MD, NY, NZ), F32)
    own, other = pl.pallas_call(
        kernel,
        out_shape=(plane, plane),
        in_specs=[hbm] * 4,
        out_specs=(hbm, hbm),
        scratch_shapes=[
            vmem((NX, MP, NY, NZ), F32),
            vmem((KT, NY, NZ), F32),
            vmem((KT, NY, NZ), F32),
            vmem((KT, NY, NZ), F32),
            vmem((KT, NY, NZ), F32),
            vmem((KT - 1, NY, NY), F32),
            vmem((5, KT, 128, NZ), F32),
            vmem((KT * OUT2, KD), BF16),
            vmem((2, MP, PR, NZ), F32),
            vmem((2, MP, NY, NZ), F32),
            vmem((2, MP, NY, NZ), F32),
            vmem((2, MP, NY, NZ), F32),
            vmem((2, MP, NY, NZ), F32),
            vmem((2, MP, NY, NZ), F32),
            vmem((2, OUT2, NZ), F32),
            dma((4,)), dma((NC,)),
            dma((3, NC)), dma((3, NC)),
            dma((2, NC)), dma((2, NC)),
            dma((NC,)), dma((NC,)),
            dma((NC,)), dma((NC,)),
            dma((2, KT)), dma((2, KT)),
            dma((KT,)), dma((KT,)),
        ],
        compiler_params=pltpu.CompilerParams(
            collective_id=0, has_side_effects=True, vmem_limit_bytes=56 * 1024 * 1024
        ),
    )(mode_coeffs.reshape(MD, NY, NZ), mean_perm.reshape(NY, NZ), kl_fields.reshape(KT - 1, NY, NZ), couplings)
    return (own + other).reshape(MD, 1, NY, NZ)


def solution(mesh):
    in_specs = (
        P("modes", "space", None, None),
        P("space", None, None),
        P(None, "space", None, None),
        P(),
    )
    out_specs = P("modes", "space", None, None)
    return jax.shard_map(local, mesh=mesh, in_specs=in_specs, out_specs=out_specs, check_vma=False)
```

```python
import functools

import jax
import jax.numpy as jnp
from jax import lax
from jax.experimental import pallas as pl
from jax.experimental.pallas import tpu as pltpu
from jax.sharding import PartitionSpec as P

MESH = pl.DeviceIdType.MESH
F32, BF16 = jnp.float32, jnp.bfloat16

MD = 15
MP = 16
NX = 4
NY, NZ = 120, 128
KT = 8
R = 8
NC = NY // R
LINE = 8
OUT2 = 2 * MP
PR = NY + 16
KD = 3 * NX * MP
BACK = 2
LATE = 4
SEAM = 0
AHEAD = 3
LAG = 2


def kernel(u, mean, kl, cpl, out, zr, gath, fld, flo, fhi, rfl, cplv, cf, w, part, tlo, thi, hlo, hhi, rel,
           carry, sem_l, sem_o, sx_s, sx_r, sh_s, sh_r, sr_s, sr_r, sz_s, sz_r, ff_s, ff_r, fr_s, fr_r):
    m = lax.axis_index("modes")
    s = lax.axis_index("space")
    x = lax.rem(m, NX)
    zhi = m // NX
    first, last = s == 0, s == 31
    xr = zhi * NX + lax.rem(x + 1, NX)
    xl = zhi * NX + lax.rem(x + NX - 1, NX)
    zp = lax.rem(m + NX, 2 * NX)

    xf = zhi * NX + lax.rem(x + 2, NX)

    y, core, zlo = lax.rem(s, LINE) // 2, lax.rem(s, 2), s // LINE
    line = zlo * LINE
    up, down = jnp.logical_not(last), jnp.logical_not(first)
    seam_up = (core == 1) & (y == 3) & (zlo < 3)
    seam_down = (core == 0) & (y == 0) & (zlo > 0)
    relay_up = (core == 1) & (y == 0) & (zlo < 3)
    relay_down = (core == 0) & (y == 3) & (zlo > 0)
    seam, relay = seam_up | seam_down, relay_up | relay_down
    goal = jnp.where(core == 1, line + LINE, line - 1)
    origin = jnp.where(core == 1, line + LINE - 1, line)
    aside = jnp.where(core == 1, line + 1, line + LINE - 2)

    barrier = pltpu.get_barrier_semaphore()

    def greet(dev):
        pl.semaphore_signal(barrier, inc=1, device_id=dev, device_id_type=MESH)

    greet((xr, s))
    greet((xl, s))
    greet((xf, s))
    greet((zp, s))

    @pl.when(down)
    def _():
        greet((m, s - 1))

    @pl.when(up)
    def _():
        greet((m, s + 1))

    @pl.when(relay)
    def _():
        greet((m, origin))

    @pl.when(seam_down)
    def _():
        greet((m, line - LINE + 1))
        greet((m, aside))

    @pl.when(seam_up)
    def _():
        greet((m, line + LINE + LINE - 2))
        greet((m, aside))

    local = [
        pltpu.make_async_copy(u, gath.at[x, 0:MD], sem_l.at[0]),
        pltpu.make_async_copy(mean, fld.at[0], sem_l.at[1]),
        pltpu.make_async_copy(kl, fld.at[1:KT], sem_l.at[2]),
        pltpu.make_async_copy(cpl, cplv, sem_l.at[3]),
    ]
    for copy in local:
        copy.start()

    gath[:, MD] = jnp.zeros((NX, NY, NZ), F32)

    @pl.when(first)
    def _():
        flo[...] = jnp.zeros(flo.shape, F32)
        hlo[...] = jnp.zeros(hlo.shape, F32)

    @pl.when(last)
    def _():
        fhi[...] = jnp.zeros(fhi.shape, F32)
        hhi[...] = jnp.zeros(hhi.shape, F32)

    carry[...] = jnp.zeros(carry.shape, F32)

    one = jnp.int32
    lag = LAG + SEAM * seam.astype(one)
    pl.semaphore_wait(barrier, 4 + up.astype(one) + down.astype(one) + 2 * relay.astype(one) + seam.astype(one))

    def remote(src, dst, send, recv, dev):
        return pltpu.make_async_remote_copy(
            src_ref=src, dst_ref=dst, send_sem=send, recv_sem=recv, device_id=dev, device_id_type=MESH
        )

    def rows(c, base=0):
        return pl.ds(pl.multiple_of(base + c * R, R), R)

    x_from = [lax.rem(x + NX - 1, NX), lax.rem(x + 1, NX), lax.rem(x + 2, NX)]
    x_to = [xr, xl, xf]

    def own(i, c):
        return remote(u.at[:, rows(c)], gath.at[x, 0:MD, rows(c)], sx_s.at[i, c], sx_r.at[i, c], (x_to[i], s))

    def got(i, c):
        ref = gath.at[x_from[i], 0:MD, rows(c)]
        return remote(ref, ref, sx_s.at[i, c], sx_r.at[i, c], (x_to[i], s))

    def field(k):
        return mean if k == 0 else kl.at[k - 1]

    def field_up(k):
        return remote(field(k), flo.at[k], ff_s.at[0, k], ff_r.at[0, k], (m, s + 1))

    def field_down(k):
        return remote(field(k), fhi.at[k], ff_s.at[1, k], ff_r.at[1, k], (m, s - 1))

    def field_aside(k):
        return remote(field(k), rfl.at[k], ff_s.at[core ^ 1, k], fr_r.at[k], (m, aside))

    def field_relay_up(k):
        return remote(rfl.at[k], flo.at[k], fr_s.at[k], ff_r.at[0, k], (m, goal))

    def field_relay_down(k):
        return remote(rfl.at[k], fhi.at[k], fr_s.at[k], ff_r.at[1, k], (m, goal))

    def halo_up(o, c):
        return remote(thi.at[o, 0:MD, rows(c)], hlo.at[o, 0:MD, rows(c)], sh_s.at[o, c], sh_r.at[o, c], (m, s + 1))

    def halo_down(o, c):
        return remote(tlo.at[o, 0:MD, rows(c)], hhi.at[o, 0:MD, rows(c)], sh_s.at[2 + o, c], sh_r.at[2 + o, c], (m, s - 1))

    def aside_up(o, c):
        return remote(thi.at[o, 0:MD, rows(c)], rel.at[o, 0:MD, rows(c)], sh_s.at[o, c], sr_r.at[o, c], (m, aside))

    def aside_down(o, c):
        return remote(tlo.at[o, 0:MD, rows(c)], rel.at[o, 0:MD, rows(c)], sh_s.at[2 + o, c], sr_r.at[o, c], (m, aside))

    def relay_on_up(o, c):
        return remote(rel.at[o, 0:MD, rows(c)], hlo.at[o, 0:MD, rows(c)], sr_s.at[o, c], sh_r.at[o, c], (m, goal))

    def relay_on_down(o, c):
        return remote(rel.at[o, 0:MD, rows(c)], hhi.at[o, 0:MD, rows(c)], sr_s.at[o, c], sh_r.at[2 + o, c], (m, goal))

    def across(c):
        return remote(part.at[1, 0:MD, rows(c, R)], zr.at[:, rows(c)], sz_s.at[c], sz_r.at[c], (zp, s))

    def keep(c):
        return pltpu.make_async_copy(part.at[0, 0:MD, rows(c, R)], out.at[:, rows(c)], sem_o.at[c])

    def when(cond, fn):
        pl.when(cond)(fn)

    for k in range(KT):
        direct_up, direct_down = up, down
        if k % 2 == 0:
            direct_up, direct_down = up & jnp.logical_not(seam_up), down & jnp.logical_not(seam_down)
            when(seam, lambda: field_aside(k).start())
        when(direct_up, lambda: field_up(k).start())
        when(direct_down, lambda: field_down(k).start())

    def gather(c, _):
        for i in range(3):
            own(i, c).start()
        return 0

    lax.fori_loop(0, AHEAD, gather, 0)

    local[3].wait()
    ri = lax.broadcasted_iota(jnp.int32, (OUT2, NY), 0)
    rc = lax.broadcasted_iota(jnp.int32, (OUT2, NY), 1)
    ro, rm = ri // MP, lax.rem(ri, MP)
    row_of = jnp.where(ro == 0, m, zp) * MD + rm
    pick = jnp.where((rc == row_of) & (rm < MD), 1.0, 0.0).astype(BF16)
    ci = lax.broadcasted_iota(jnp.int32, (NY, KD), 0)
    cj = lax.broadcasted_iota(jnp.int32, (NY, KD), 1)
    blk, cs = cj // (NX * MP), lax.rem(cj, NX * MP)
    cm = lax.rem(cs, MP)
    hit = (ci == zhi * (NX * MD) + (cs // MP) * MD + cm) & (cm < MD)
    put_hi = jnp.where(hit & (blk < 2), 1.0, 0.0).astype(BF16)
    put_lo = jnp.where(hit & (blk == 2), 1.0, 0.0).astype(BF16)
    di = lax.broadcasted_iota(jnp.int32, (OUT2, KD), 0)
    dj = lax.broadcasted_iota(jnp.int32, (OUT2, KD), 1)
    same = (di < MD) & (dj < 2 * NX * MP) & (lax.rem(dj, NX * MP) == x * MP + di)
    w[0:OUT2] = jnp.where(same, 1.0, 0.0).astype(BF16)

    def dot(a, b):
        return jnp.dot(a, b, preferred_element_type=F32)

    for k in range(1, KT):
        full = cplv[k - 1]
        hi = full.astype(BF16)
        lo = (full - hi.astype(F32)).astype(BF16)
        rows_hi = dot(pick, hi).astype(BF16)
        rows_lo = dot(pick, lo).astype(BF16)
        w[k * OUT2:(k + 1) * OUT2] = (dot(rows_hi, put_hi) + dot(rows_lo, put_lo)).astype(BF16)

    local[1].wait()
    local[2].wait()
    lane = lax.broadcasted_iota(jnp.int32, (NY, NZ), 1)
    none = jnp.zeros((1, NZ), F32)
    for k in range(KT):
        a = fld[k]
        cf[2, k, 0:NY + 1] = 0.5 * (jnp.concatenate([none, a], 0) + jnp.concatenate([a, none], 0))
        cf[3, k, 0:NY] = 0.5 * (a + jnp.where(lane == 0, 0.0, pltpu.roll(a, 1, 1)))
        cf[4, k, 0:NY] = 0.5 * (a + jnp.where(lane == NZ - 1, 0.0, pltpu.roll(a, NZ - 1, 1)))

    for k in range(0, KT, 2):
        @pl.when(relay)
        def _():
            field_aside(k).wait_recv()
            when(core == 1, lambda: field_relay_up(k).start())
            when(core == 0, lambda: field_relay_down(k).start())

    for k in range(KT):
        when(down, lambda: field_up(k).wait_recv())
        when(up, lambda: field_down(k).wait_recv())

    for k in range(KT):
        cf[0, k, 0:NY] = 0.5 * (fld[k] + flo[k])
        cf[1, k, 0:NY] = 0.5 * (fld[k] + fhi[k])

    local[0].wait()

    gflat = gath.reshape(NX * MP * NY, NZ)
    pflat = part.reshape(OUT2 * PR, NZ)
    tlo_flat = tlo.reshape(OUT2 * NY, NZ)
    thi_flat = thi.reshape(OUT2 * NY, NZ)
    lane2 = lax.broadcasted_iota(jnp.int32, (OUT2, NZ), 1)

    def compute(c):
        def pair(q, held):
            acc, above = held
            r0 = c * R + 2 * q
            cols = []
            for a in range(2):
                xf = gflat[pl.ds(r0 + a, NX * MP, stride=NY), :]
                hi = xf.astype(BF16)
                lo = (xf - hi.astype(F32)).astype(BF16)
                cols.append(jnp.concatenate([hi, lo, hi], 0))
            v = dot(w[...], jnp.concatenate(cols, 1))
            for a in range(2):
                r = r0 + a
                sums = [None] * 6
                for k in range(KT):
                    vk = v[k * OUT2:(k + 1) * OUT2, a * NZ:(a + 1) * NZ]
                    for d, (kind, at) in enumerate(((0, 0), (1, 0), (2, 0), (2, 1), (3, 0), (4, 0))):
                        term = cf[kind, k, pl.ds(r + at, 1), :] * vk
                        sums[d] = term if sums[d] is None else sums[d] + term
                xlo, xhi, ylo, yhi, zlo, zhi_ = sums
                tlo_flat[pl.ds(r, OUT2, stride=NY), :] = xlo
                thi_flat[pl.ds(r, OUT2, stride=NY), :] = xhi
                pflat[pl.ds(r + R - 1, OUT2, stride=PR), :] = acc - ylo
                acc = ((xlo + xhi) + (ylo + yhi)) + (zlo + zhi_) - above
                acc = acc - jnp.where(lane2 == 0, 0.0, pltpu.roll(zhi_, 1, 1))
                acc = acc - jnp.where(lane2 == NZ - 1, 0.0, pltpu.roll(zlo, NZ - 1, 1))
                above = yhi
            return acc, above

        acc, above = lax.fori_loop(0, R // 2, pair, (carry[0], carry[1]))
        carry[0] = acc
        carry[1] = above

    def send_halos(c):
        when(up, lambda: halo_up(1, c).start())
        when(down, lambda: halo_down(1, c).start())
        when(up & jnp.logical_not(seam_up), lambda: halo_up(0, c).start())
        when(down & jnp.logical_not(seam_down), lambda: halo_down(0, c).start())
        when(seam_up, lambda: aside_up(0, c).start())
        when(seam_down, lambda: aside_down(0, c).start())

    def join(o, c):
        when(down, lambda: halo_up(o, c).wait_recv())
        when(up, lambda: halo_down(o, c).wait_recv())
        here = part[o, 0:MD, rows(c, R)]
        part[o, 0:MD, rows(c, R)] = here - (hlo[o, 0:MD, rows(c)] + hhi[o, 0:MD, rows(c)])

    def step(t, _):
        @pl.when(t + AHEAD < NC)
        def _():
            gather(t + AHEAD, 0)

        @pl.when(t < NC)
        def _():
            for i in range(3):
                got(i, t).wait_recv()

        @pl.when((t >= BACK) & (t < NC + BACK) & relay)
        def _():
            c = t - BACK
            aside_up(0, c).wait_recv()
            when(core == 1, lambda: relay_on_up(0, c).start())
            when(core == 0, lambda: relay_on_down(0, c).start())

        @pl.when(t < NC)
        def _():
            compute(t)
            send_halos(t)

            @pl.when(t == NC - 1)
            def _():
                pflat[pl.ds(NY - 1 + R, OUT2, stride=PR), :] = carry[0]

        @pl.when((t >= lag) & (t < NC + lag))
        def _():
            c = t - lag
            join(1, c)
            across(c).start()

        @pl.when((t >= lag + LATE) & (t < NC + lag + LATE))
        def _():
            c = t - lag - LATE
            join(0, c)
            keep(c).start()

        return 0

    lax.fori_loop(0, NC + LAG + SEAM + LATE, step, 0)

    def drain(c, _):
        for i in range(3):
            own(i, c).wait_send()
        for o in range(2):
            when(up, lambda: halo_up(o, c).wait_send())
            when(down, lambda: halo_down(o, c).wait_send())
        keep(c).wait()
        when(relay, lambda: relay_on_up(0, c).wait_send())
        across(c).wait_send()
        across(c).wait_recv()
        return 0

    for k in range(KT):
        when(up, lambda: field_up(k).wait_send())
        when(down, lambda: field_down(k).wait_send())
        if k % 2 == 0:
            when(relay, lambda: field_relay_up(k).wait_send())

    lax.fori_loop(0, NC, drain, 0)


def local(mode_coeffs, mean_perm, kl_fields, couplings):
    dma = pltpu.SemaphoreType.DMA
    hbm = pl.BlockSpec(memory_space=pl.ANY)
    vmem = pltpu.VMEM
    plane = jax.ShapeDtypeStruct((MD, NY, NZ), F32)
    own, other = pl.pallas_call(
        kernel,
        out_shape=(plane, plane),
        in_specs=[hbm] * 4,
        out_specs=(hbm, hbm),
        scratch_shapes=[
            vmem((NX, MP, NY, NZ), F32),
            vmem((KT, NY, NZ), F32),
            vmem((KT, NY, NZ), F32),
            vmem((KT, NY, NZ), F32),
            vmem((KT, NY, NZ), F32),
            vmem((KT - 1, NY, NY), F32),
            vmem((5, KT, 128, NZ), F32),
            vmem((KT * OUT2, KD), BF16),
            vmem((2, MP, PR, NZ), F32),
            vmem((2, MP, NY, NZ), F32),
            vmem((2, MP, NY, NZ), F32),
            vmem((2, MP, NY, NZ), F32),
            vmem((2, MP, NY, NZ), F32),
            vmem((2, MP, NY, NZ), F32),
            vmem((2, OUT2, NZ), F32),
            dma((4,)), dma((NC,)),
            dma((3, NC)), dma((3, NC)),
            dma((4, NC)), dma((4, NC)),
            dma((2, NC)), dma((2, NC)),
            dma((NC,)), dma((NC,)),
            dma((2, KT)), dma((2, KT)),
            dma((KT,)), dma((KT,)),
        ],
        compiler_params=pltpu.CompilerParams(
            collective_id=0, has_side_effects=True, vmem_limit_bytes=56 * 1024 * 1024
        ),
    )(mode_coeffs.reshape(MD, NY, NZ), mean_perm.reshape(NY, NZ), kl_fields.reshape(KT - 1, NY, NZ), couplings)
    return (own + other).reshape(MD, 1, NY, NZ)


def solution(mesh):
    in_specs = (
        P("modes", "space", None, None),
        P("space", None, None),
        P(None, "space", None, None),
        P(),
    )
    out_specs = P("modes", "space", None, None)
    return jax.shard_map(local, mesh=mesh, in_specs=in_specs, out_specs=out_specs, check_vma=False)
```

```python
import functools

import jax
import jax.numpy as jnp
from jax import lax
from jax.experimental import pallas as pl
from jax.experimental.pallas import tpu as pltpu
from jax.sharding import PartitionSpec as P

MESH = pl.DeviceIdType.MESH
F32, BF16 = jnp.float32, jnp.bfloat16

MD = 15
MP = 16
NX = 4
NY, NZ = 120, 128
KT = 8
R = 8
NC = NY // R
LINE = 8
OUT2 = 2 * MP
PR = NY + 16
KD = 3 * NX * MP
BACK = 3
LATE = 6
SEAM = 0
AHEAD = 3
LAG = 2


def kernel(u, mean, kl, cpl, out, zr, gath, fld, flo, fhi, rfl, cplv, cf, w, part, tlo, thi, hlo, hhi, rel,
           carry, sem_l, sem_o, sx_s, sx_r, sh_s, sh_r, sr_s, sr_r, sz_s, sz_r, ff_s, ff_r, fr_s, fr_r):
    m = lax.axis_index("modes")
    s = lax.axis_index("space")
    x = lax.rem(m, NX)
    zhi = m // NX
    first, last = s == 0, s == 31
    xr = zhi * NX + lax.rem(x + 1, NX)
    xl = zhi * NX + lax.rem(x + NX - 1, NX)
    zp = lax.rem(m + NX, 2 * NX)

    xf = zhi * NX + lax.rem(x + 2, NX)

    y, core, zlo = lax.rem(s, LINE) // 2, lax.rem(s, 2), s // LINE
    line = zlo * LINE
    up, down = jnp.logical_not(last), jnp.logical_not(first)
    seam_up = (core == 1) & (y == 3) & (zlo < 3)
    seam_down = (core == 0) & (y == 0) & (zlo > 0)
    relay_up = (core == 1) & (y == 0) & (zlo < 3)
    relay_down = (core == 0) & (y == 3) & (zlo > 0)
    seam, relay = seam_up | seam_down, relay_up | relay_down
    goal = jnp.where(core == 1, line + LINE, line - 1)
    origin = jnp.where(core == 1, line + LINE - 1, line)
    aside = jnp.where(core == 1, line + 1, line + LINE - 2)

    barrier = pltpu.get_barrier_semaphore()

    def greet(dev):
        pl.semaphore_signal(barrier, inc=1, device_id=dev, device_id_type=MESH)

    greet((xr, s))
    greet((xl, s))
    greet((xf, s))
    greet((zp, s))

    @pl.when(down)
    def _():
        greet((m, s - 1))

    @pl.when(up)
    def _():
        greet((m, s + 1))

    @pl.when(relay)
    def _():
        greet((m, origin))

    @pl.when(seam_down)
    def _():
        greet((m, line - LINE + 1))
        greet((m, aside))

    @pl.when(seam_up)
    def _():
        greet((m, line + LINE + LINE - 2))
        greet((m, aside))

    local = [
        pltpu.make_async_copy(u, gath.at[x, 0:MD], sem_l.at[0]),
        pltpu.make_async_copy(mean, fld.at[0], sem_l.at[1]),
        pltpu.make_async_copy(kl, fld.at[1:KT], sem_l.at[2]),
        pltpu.make_async_copy(cpl, cplv, sem_l.at[3]),
    ]
    for copy in local:
        copy.start()

    gath[:, MD] = jnp.zeros((NX, NY, NZ), F32)

    @pl.when(first)
    def _():
        flo[...] = jnp.zeros(flo.shape, F32)
        hlo[...] = jnp.zeros(hlo.shape, F32)

    @pl.when(last)
    def _():
        fhi[...] = jnp.zeros(fhi.shape, F32)
        hhi[...] = jnp.zeros(hhi.shape, F32)

    carry[...] = jnp.zeros(carry.shape, F32)

    one = jnp.int32
    lag = LAG + SEAM * seam.astype(one)
    pl.semaphore_wait(barrier, 4 + up.astype(one) + down.astype(one) + 2 * relay.astype(one) + seam.astype(one))

    def remote(src, dst, send, recv, dev):
        return pltpu.make_async_remote_copy(
            src_ref=src, dst_ref=dst, send_sem=send, recv_sem=recv, device_id=dev, device_id_type=MESH
        )

    def rows(c, base=0):
        return pl.ds(pl.multiple_of(base + c * R, R), R)

    x_from = [lax.rem(x + NX - 1, NX), lax.rem(x + 1, NX), lax.rem(x + 2, NX)]
    x_to = [xr, xl, xf]

    def own(i, c):
        return remote(u.at[:, rows(c)], gath.at[x, 0:MD, rows(c)], sx_s.at[i, c], sx_r.at[i, c], (x_to[i], s))

    def got(i, c):
        ref = gath.at[x_from[i], 0:MD, rows(c)]
        return remote(ref, ref, sx_s.at[i, c], sx_r.at[i, c], (x_to[i], s))

    def field(k):
        return mean if k == 0 else kl.at[k - 1]

    def field_up(k):
        return remote(field(k), flo.at[k], ff_s.at[0, k], ff_r.at[0, k], (m, s + 1))

    def field_down(k):
        return remote(field(k), fhi.at[k], ff_s.at[1, k], ff_r.at[1, k], (m, s - 1))

    def field_aside(k):
        return remote(field(k), rfl.at[k], ff_s.at[core ^ 1, k], fr_r.at[k], (m, aside))

    def field_relay_up(k):
        return remote(rfl.at[k], flo.at[k], fr_s.at[k], ff_r.at[0, k], (m, goal))

    def field_relay_down(k):
        return remote(rfl.at[k], fhi.at[k], fr_s.at[k], ff_r.at[1, k], (m, goal))

    def halo_up(o, c):
        return remote(thi.at[o, 0:MD, rows(c)], hlo.at[o, 0:MD, rows(c)], sh_s.at[o, c], sh_r.at[o, c], (m, s + 1))

    def halo_down(o, c):
        return remote(tlo.at[o, 0:MD, rows(c)], hhi.at[o, 0:MD, rows(c)], sh_s.at[2 + o, c], sh_r.at[2 + o, c], (m, s - 1))

    def aside_up(o, c):
        return remote(thi.at[o, 0:MD, rows(c)], rel.at[o, 0:MD, rows(c)], sh_s.at[o, c], sr_r.at[o, c], (m, aside))

    def aside_down(o, c):
        return remote(tlo.at[o, 0:MD, rows(c)], rel.at[o, 0:MD, rows(c)], sh_s.at[2 + o, c], sr_r.at[o, c], (m, aside))

    def relay_on_up(o, c):
        return remote(rel.at[o, 0:MD, rows(c)], hlo.at[o, 0:MD, rows(c)], sr_s.at[o, c], sh_r.at[o, c], (m, goal))

    def relay_on_down(o, c):
        return remote(rel.at[o, 0:MD, rows(c)], hhi.at[o, 0:MD, rows(c)], sr_s.at[o, c], sh_r.at[2 + o, c], (m, goal))

    def across(c):
        return remote(part.at[1, 0:MD, rows(c, R)], zr.at[:, rows(c)], sz_s.at[c], sz_r.at[c], (zp, s))

    def keep(c):
        return pltpu.make_async_copy(part.at[0, 0:MD, rows(c, R)], out.at[:, rows(c)], sem_o.at[c])

    def when(cond, fn):
        pl.when(cond)(fn)

    for k in range(KT):
        direct_up, direct_down = up, down
        if k % 2 == 0:
            direct_up, direct_down = up & jnp.logical_not(seam_up), down & jnp.logical_not(seam_down)
            when(seam, lambda: field_aside(k).start())
        when(direct_up, lambda: field_up(k).start())
        when(direct_down, lambda: field_down(k).start())

    def gather(c, _):
        for i in range(3):
            own(i, c).start()
        return 0

    lax.fori_loop(0, AHEAD, gather, 0)

    local[3].wait()
    ri = lax.broadcasted_iota(jnp.int32, (OUT2, NY), 0)
    rc = lax.broadcasted_iota(jnp.int32, (OUT2, NY), 1)
    ro, rm = ri // MP, lax.rem(ri, MP)
    row_of = jnp.where(ro == 0, m, zp) * MD + rm
    pick = jnp.where((rc == row_of) & (rm < MD), 1.0, 0.0).astype(BF16)
    ci = lax.broadcasted_iota(jnp.int32, (NY, KD), 0)
    cj = lax.broadcasted_iota(jnp.int32, (NY, KD), 1)
    blk, cs = cj // (NX * MP), lax.rem(cj, NX * MP)
    cm = lax.rem(cs, MP)
    hit = (ci == zhi * (NX * MD) + (cs // MP) * MD + cm) & (cm < MD)
    put_hi = jnp.where(hit & (blk < 2), 1.0, 0.0).astype(BF16)
    put_lo = jnp.where(hit & (blk == 2), 1.0, 0.0).astype(BF16)
    di = lax.broadcasted_iota(jnp.int32, (OUT2, KD), 0)
    dj = lax.broadcasted_iota(jnp.int32, (OUT2, KD), 1)
    same = (di < MD) & (dj < 2 * NX * MP) & (lax.rem(dj, NX * MP) == x * MP + di)
    w[0:OUT2] = jnp.where(same, 1.0, 0.0).astype(BF16)

    def dot(a, b):
        return jnp.dot(a, b, preferred_element_type=F32)

    for k in range(1, KT):
        full = cplv[k - 1]
        hi = full.astype(BF16)
        lo = (full - hi.astype(F32)).astype(BF16)
        rows_hi = dot(pick, hi).astype(BF16)
        rows_lo = dot(pick, lo).astype(BF16)
        w[k * OUT2:(k + 1) * OUT2] = (dot(rows_hi, put_hi) + dot(rows_lo, put_lo)).astype(BF16)

    local[1].wait()
    local[2].wait()
    lane = lax.broadcasted_iota(jnp.int32, (NY, NZ), 1)
    none = jnp.zeros((1, NZ), F32)
    for k in range(KT):
        a = fld[k]
        cf[2, k, 0:NY + 1] = 0.5 * (jnp.concatenate([none, a], 0) + jnp.concatenate([a, none], 0))
        cf[3, k, 0:NY] = 0.5 * (a + jnp.where(lane == 0, 0.0, pltpu.roll(a, 1, 1)))
        cf[4, k, 0:NY] = 0.5 * (a + jnp.where(lane == NZ - 1, 0.0, pltpu.roll(a, NZ - 1, 1)))

    for k in range(0, KT, 2):
        @pl.when(relay)
        def _():
            field_aside(k).wait_recv()
            when(core == 1, lambda: field_relay_up(k).start())
            when(core == 0, lambda: field_relay_down(k).start())

    for k in range(KT):
        when(down, lambda: field_up(k).wait_recv())
        when(up, lambda: field_down(k).wait_recv())

    for k in range(KT):
        cf[0, k, 0:NY] = 0.5 * (fld[k] + flo[k])
        cf[1, k, 0:NY] = 0.5 * (fld[k] + fhi[k])

    local[0].wait()

    gflat = gath.reshape(NX * MP * NY, NZ)
    pflat = part.reshape(OUT2 * PR, NZ)
    tlo_flat = tlo.reshape(OUT2 * NY, NZ)
    thi_flat = thi.reshape(OUT2 * NY, NZ)
    lane2 = lax.broadcasted_iota(jnp.int32, (OUT2, NZ), 1)

    def compute(c):
        def pair(q, held):
            acc, above = held
            r0 = c * R + 2 * q
            cols = []
            for a in range(2):
                xf = gflat[pl.ds(r0 + a, NX * MP, stride=NY), :]
                hi = xf.astype(BF16)
                lo = (xf - hi.astype(F32)).astype(BF16)
                cols.append(jnp.concatenate([hi, lo, hi], 0))
            v = dot(w[...], jnp.concatenate(cols, 1))
            for a in range(2):
                r = r0 + a
                sums = [None] * 6
                for k in range(KT):
                    vk = v[k * OUT2:(k + 1) * OUT2, a * NZ:(a + 1) * NZ]
                    for d, (kind, at) in enumerate(((0, 0), (1, 0), (2, 0), (2, 1), (3, 0), (4, 0))):
                        term = cf[kind, k, pl.ds(r + at, 1), :] * vk
                        sums[d] = term if sums[d] is None else sums[d] + term
                xlo, xhi, ylo, yhi, zlo, zhi_ = sums
                tlo_flat[pl.ds(r, OUT2, stride=NY), :] = xlo
                thi_flat[pl.ds(r, OUT2, stride=NY), :] = xhi
                pflat[pl.ds(r + R - 1, OUT2, stride=PR), :] = acc - ylo
                acc = ((xlo + xhi) + (ylo + yhi)) + (zlo + zhi_) - above
                acc = acc - jnp.where(lane2 == 0, 0.0, pltpu.roll(zhi_, 1, 1))
                acc = acc - jnp.where(lane2 == NZ - 1, 0.0, pltpu.roll(zlo, NZ - 1, 1))
                above = yhi
            return acc, above

        acc, above = lax.fori_loop(0, R // 2, pair, (carry[0], carry[1]))
        carry[0] = acc
        carry[1] = above

    def send_halos(c):
        when(up, lambda: halo_up(1, c).start())
        when(down, lambda: halo_down(1, c).start())
        when(up & jnp.logical_not(seam_up), lambda: halo_up(0, c).start())
        when(down & jnp.logical_not(seam_down), lambda: halo_down(0, c).start())
        when(seam_up, lambda: aside_up(0, c).start())
        when(seam_down, lambda: aside_down(0, c).start())

    def join(o, c):
        when(down, lambda: halo_up(o, c).wait_recv())
        when(up, lambda: halo_down(o, c).wait_recv())
        here = part[o, 0:MD, rows(c, R)]
        part[o, 0:MD, rows(c, R)] = here - (hlo[o, 0:MD, rows(c)] + hhi[o, 0:MD, rows(c)])

    def step(t, _):
        @pl.when(t + AHEAD < NC)
        def _():
            gather(t + AHEAD, 0)

        @pl.when(t < NC)
        def _():
            for i in range(3):
                got(i, t).wait_recv()

        @pl.when((t >= BACK) & (t < NC + BACK) & relay)
        def _():
            c = t - BACK
            aside_up(0, c).wait_recv()
            when(core == 1, lambda: relay_on_up(0, c).start())
            when(core == 0, lambda: relay_on_down(0, c).start())

        @pl.when(t < NC)
        def _():
            compute(t)
            send_halos(t)

            @pl.when(t == NC - 1)
            def _():
                pflat[pl.ds(NY - 1 + R, OUT2, stride=PR), :] = carry[0]

        @pl.when((t >= lag) & (t < NC + lag))
        def _():
            c = t - lag
            join(1, c)
            across(c).start()

        @pl.when((t >= lag + LATE) & (t < NC + lag + LATE))
        def _():
            c = t - lag - LATE
            join(0, c)
            keep(c).start()

        return 0

    lax.fori_loop(0, NC + LAG + SEAM + LATE, step, 0)

    def drain(c, _):
        for i in range(3):
            own(i, c).wait_send()
        for o in range(2):
            when(up, lambda: halo_up(o, c).wait_send())
            when(down, lambda: halo_down(o, c).wait_send())
        keep(c).wait()
        when(relay, lambda: relay_on_up(0, c).wait_send())
        across(c).wait_send()
        across(c).wait_recv()
        return 0

    for k in range(KT):
        when(up, lambda: field_up(k).wait_send())
        when(down, lambda: field_down(k).wait_send())
        if k % 2 == 0:
            when(relay, lambda: field_relay_up(k).wait_send())

    lax.fori_loop(0, NC, drain, 0)


def local(mode_coeffs, mean_perm, kl_fields, couplings):
    dma = pltpu.SemaphoreType.DMA
    hbm = pl.BlockSpec(memory_space=pl.ANY)
    vmem = pltpu.VMEM
    plane = jax.ShapeDtypeStruct((MD, NY, NZ), F32)
    own, other = pl.pallas_call(
        kernel,
        out_shape=(plane, plane),
        in_specs=[hbm] * 4,
        out_specs=(hbm, hbm),
        scratch_shapes=[
            vmem((NX, MP, NY, NZ), F32),
            vmem((KT, NY, NZ), F32),
            vmem((KT, NY, NZ), F32),
            vmem((KT, NY, NZ), F32),
            vmem((KT, NY, NZ), F32),
            vmem((KT - 1, NY, NY), F32),
            vmem((5, KT, 128, NZ), F32),
            vmem((KT * OUT2, KD), BF16),
            vmem((2, MP, PR, NZ), F32),
            vmem((2, MP, NY, NZ), F32),
            vmem((2, MP, NY, NZ), F32),
            vmem((2, MP, NY, NZ), F32),
            vmem((2, MP, NY, NZ), F32),
            vmem((2, MP, NY, NZ), F32),
            vmem((2, OUT2, NZ), F32),
            dma((4,)), dma((NC,)),
            dma((3, NC)), dma((3, NC)),
            dma((4, NC)), dma((4, NC)),
            dma((2, NC)), dma((2, NC)),
            dma((NC,)), dma((NC,)),
            dma((2, KT)), dma((2, KT)),
            dma((KT,)), dma((KT,)),
        ],
        compiler_params=pltpu.CompilerParams(
            collective_id=0, has_side_effects=True, vmem_limit_bytes=56 * 1024 * 1024
        ),
    )(mode_coeffs.reshape(MD, NY, NZ), mean_perm.reshape(NY, NZ), kl_fields.reshape(KT - 1, NY, NZ), couplings)
    return (own + other).reshape(MD, 1, NY, NZ)


def solution(mesh):
    in_specs = (
        P("modes", "space", None, None),
        P("space", None, None),
        P(None, "space", None, None),
        P(),
    )
    out_specs = P("modes", "space", None, None)
    return jax.shard_map(local, mesh=mesh, in_specs=in_specs, out_specs=out_specs, check_vma=False)
```

```python
import functools

import jax
import jax.numpy as jnp
from jax import lax
from jax.experimental import pallas as pl
from jax.experimental.pallas import tpu as pltpu
from jax.sharding import PartitionSpec as P

MESH = pl.DeviceIdType.MESH
F32, BF16 = jnp.float32, jnp.bfloat16

MD = 15
MP = 16
NX = 4
NY, NZ = 120, 128
KT = 8
R = 8
NC = NY // R
LINE = 8
OUT2 = 2 * MP
PR = NY + 16
KD = 3 * NX * MP
BACK = 4
LATE = 8
SEAM = 0
AHEAD = 3
LAG = 2


def kernel(u, mean, kl, cpl, out, zr, gath, fld, flo, fhi, rfl, cplv, cf, w, part, tlo, thi, hlo, hhi, rel,
           carry, sem_l, sem_o, sx_s, sx_r, sh_s, sh_r, sr_s, sr_r, sz_s, sz_r, ff_s, ff_r, fr_s, fr_r):
    m = lax.axis_index("modes")
    s = lax.axis_index("space")
    x = lax.rem(m, NX)
    zhi = m // NX
    first, last = s == 0, s == 31
    xr = zhi * NX + lax.rem(x + 1, NX)
    xl = zhi * NX + lax.rem(x + NX - 1, NX)
    zp = lax.rem(m + NX, 2 * NX)

    xf = zhi * NX + lax.rem(x + 2, NX)

    y, core, zlo = lax.rem(s, LINE) // 2, lax.rem(s, 2), s // LINE
    line = zlo * LINE
    up, down = jnp.logical_not(last), jnp.logical_not(first)
    seam_up = (core == 1) & (y == 3) & (zlo < 3)
    seam_down = (core == 0) & (y == 0) & (zlo > 0)
    relay_up = (core == 1) & (y == 0) & (zlo < 3)
    relay_down = (core == 0) & (y == 3) & (zlo > 0)
    seam, relay = seam_up | seam_down, relay_up | relay_down
    goal = jnp.where(core == 1, line + LINE, line - 1)
    origin = jnp.where(core == 1, line + LINE - 1, line)
    aside = jnp.where(core == 1, line + 1, line + LINE - 2)

    barrier = pltpu.get_barrier_semaphore()

    def greet(dev):
        pl.semaphore_signal(barrier, inc=1, device_id=dev, device_id_type=MESH)

    greet((xr, s))
    greet((xl, s))
    greet((xf, s))
    greet((zp, s))

    @pl.when(down)
    def _():
        greet((m, s - 1))

    @pl.when(up)
    def _():
        greet((m, s + 1))

    @pl.when(relay)
    def _():
        greet((m, origin))

    @pl.when(seam_down)
    def _():
        greet((m, line - LINE + 1))
        greet((m, aside))

    @pl.when(seam_up)
    def _():
        greet((m, line + LINE + LINE - 2))
        greet((m, aside))

    local = [
        pltpu.make_async_copy(u, gath.at[x, 0:MD], sem_l.at[0]),
        pltpu.make_async_copy(mean, fld.at[0], sem_l.at[1]),
        pltpu.make_async_copy(kl, fld.at[1:KT], sem_l.at[2]),
        pltpu.make_async_copy(cpl, cplv, sem_l.at[3]),
    ]
    for copy in local:
        copy.start()

    gath[:, MD] = jnp.zeros((NX, NY, NZ), F32)

    @pl.when(first)
    def _():
        flo[...] = jnp.zeros(flo.shape, F32)
        hlo[...] = jnp.zeros(hlo.shape, F32)

    @pl.when(last)
    def _():
        fhi[...] = jnp.zeros(fhi.shape, F32)
        hhi[...] = jnp.zeros(hhi.shape, F32)

    carry[...] = jnp.zeros(carry.shape, F32)

    one = jnp.int32
    lag = LAG + SEAM * seam.astype(one)
    pl.semaphore_wait(barrier, 4 + up.astype(one) + down.astype(one) + 2 * relay.astype(one) + seam.astype(one))

    def remote(src, dst, send, recv, dev):
        return pltpu.make_async_remote_copy(
            src_ref=src, dst_ref=dst, send_sem=send, recv_sem=recv, device_id=dev, device_id_type=MESH
        )

    def rows(c, base=0):
        return pl.ds(pl.multiple_of(base + c * R, R), R)

    x_from = [lax.rem(x + NX - 1, NX), lax.rem(x + 1, NX), lax.rem(x + 2, NX)]
    x_to = [xr, xl, xf]

    def own(i, c):
        return remote(u.at[:, rows(c)], gath.at[x, 0:MD, rows(c)], sx_s.at[i, c], sx_r.at[i, c], (x_to[i], s))

    def got(i, c):
        ref = gath.at[x_from[i], 0:MD, rows(c)]
        return remote(ref, ref, sx_s.at[i, c], sx_r.at[i, c], (x_to[i], s))

    def field(k):
        return mean if k == 0 else kl.at[k - 1]

    def field_up(k):
        return remote(field(k), flo.at[k], ff_s.at[0, k], ff_r.at[0, k], (m, s + 1))

    def field_down(k):
        return remote(field(k), fhi.at[k], ff_s.at[1, k], ff_r.at[1, k], (m, s - 1))

    def field_aside(k):
        return remote(field(k), rfl.at[k], ff_s.at[core ^ 1, k], fr_r.at[k], (m, aside))

    def field_relay_up(k):
        return remote(rfl.at[k], flo.at[k], fr_s.at[k], ff_r.at[0, k], (m, goal))

    def field_relay_down(k):
        return remote(rfl.at[k], fhi.at[k], fr_s.at[k], ff_r.at[1, k], (m, goal))

    def halo_up(o, c):
        return remote(thi.at[o, 0:MD, rows(c)], hlo.at[o, 0:MD, rows(c)], sh_s.at[o, c], sh_r.at[o, c], (m, s + 1))

    def halo_down(o, c):
        return remote(tlo.at[o, 0:MD, rows(c)], hhi.at[o, 0:MD, rows(c)], sh_s.at[2 + o, c], sh_r.at[2 + o, c], (m, s - 1))

    def aside_up(o, c):
        return remote(thi.at[o, 0:MD, rows(c)], rel.at[o, 0:MD, rows(c)], sh_s.at[o, c], sr_r.at[o, c], (m, aside))

    def aside_down(o, c):
        return remote(tlo.at[o, 0:MD, rows(c)], rel.at[o, 0:MD, rows(c)], sh_s.at[2 + o, c], sr_r.at[o, c], (m, aside))

    def relay_on_up(o, c):
        return remote(rel.at[o, 0:MD, rows(c)], hlo.at[o, 0:MD, rows(c)], sr_s.at[o, c], sh_r.at[o, c], (m, goal))

    def relay_on_down(o, c):
        return remote(rel.at[o, 0:MD, rows(c)], hhi.at[o, 0:MD, rows(c)], sr_s.at[o, c], sh_r.at[2 + o, c], (m, goal))

    def across(c):
        return remote(part.at[1, 0:MD, rows(c, R)], zr.at[:, rows(c)], sz_s.at[c], sz_r.at[c], (zp, s))

    def keep(c):
        return pltpu.make_async_copy(part.at[0, 0:MD, rows(c, R)], out.at[:, rows(c)], sem_o.at[c])

    def when(cond, fn):
        pl.when(cond)(fn)

    for k in range(KT):
        direct_up, direct_down = up, down
        if k % 2 == 0:
            direct_up, direct_down = up & jnp.logical_not(seam_up), down & jnp.logical_not(seam_down)
            when(seam, lambda: field_aside(k).start())
        when(direct_up, lambda: field_up(k).start())
        when(direct_down, lambda: field_down(k).start())

    def gather(c, _):
        for i in range(3):
            own(i, c).start()
        return 0

    lax.fori_loop(0, AHEAD, gather, 0)

    local[3].wait()
    ri = lax.broadcasted_iota(jnp.int32, (OUT2, NY), 0)
    rc = lax.broadcasted_iota(jnp.int32, (OUT2, NY), 1)
    ro, rm = ri // MP, lax.rem(ri, MP)
    row_of = jnp.where(ro == 0, m, zp) * MD + rm
    pick = jnp.where((rc == row_of) & (rm < MD), 1.0, 0.0).astype(BF16)
    ci = lax.broadcasted_iota(jnp.int32, (NY, KD), 0)
    cj = lax.broadcasted_iota(jnp.int32, (NY, KD), 1)
    blk, cs = cj // (NX * MP), lax.rem(cj, NX * MP)
    cm = lax.rem(cs, MP)
    hit = (ci == zhi * (NX * MD) + (cs // MP) * MD + cm) & (cm < MD)
    put_hi = jnp.where(hit & (blk < 2), 1.0, 0.0).astype(BF16)
    put_lo = jnp.where(hit & (blk == 2), 1.0, 0.0).astype(BF16)
    di = lax.broadcasted_iota(jnp.int32, (OUT2, KD), 0)
    dj = lax.broadcasted_iota(jnp.int32, (OUT2, KD), 1)
    same = (di < MD) & (dj < 2 * NX * MP) & (lax.rem(dj, NX * MP) == x * MP + di)
    w[0:OUT2] = jnp.where(same, 1.0, 0.0).astype(BF16)

    def dot(a, b):
        return jnp.dot(a, b, preferred_element_type=F32)

    for k in range(1, KT):
        full = cplv[k - 1]
        hi = full.astype(BF16)
        lo = (full - hi.astype(F32)).astype(BF16)
        rows_hi = dot(pick, hi).astype(BF16)
        rows_lo = dot(pick, lo).astype(BF16)
        w[k * OUT2:(k + 1) * OUT2] = (dot(rows_hi, put_hi) + dot(rows_lo, put_lo)).astype(BF16)

    local[1].wait()
    local[2].wait()
    lane = lax.broadcasted_iota(jnp.int32, (NY, NZ), 1)
    none = jnp.zeros((1, NZ), F32)
    for k in range(KT):
        a = fld[k]
        cf[2, k, 0:NY + 1] = 0.5 * (jnp.concatenate([none, a], 0) + jnp.concatenate([a, none], 0))
        cf[3, k, 0:NY] = 0.5 * (a + jnp.where(lane == 0, 0.0, pltpu.roll(a, 1, 1)))
        cf[4, k, 0:NY] = 0.5 * (a + jnp.where(lane == NZ - 1, 0.0, pltpu.roll(a, NZ - 1, 1)))

    for k in range(0, KT, 2):
        @pl.when(relay)
        def _():
            field_aside(k).wait_recv()
            when(core == 1, lambda: field_relay_up(k).start())
            when(core == 0, lambda: field_relay_down(k).start())

    for k in range(KT):
        when(down, lambda: field_up(k).wait_recv())
        when(up, lambda: field_down(k).wait_recv())

    for k in range(KT):
        cf[0, k, 0:NY] = 0.5 * (fld[k] + flo[k])
        cf[1, k, 0:NY] = 0.5 * (fld[k] + fhi[k])

    local[0].wait()

    gflat = gath.reshape(NX * MP * NY, NZ)
    pflat = part.reshape(OUT2 * PR, NZ)
    tlo_flat = tlo.reshape(OUT2 * NY, NZ)
    thi_flat = thi.reshape(OUT2 * NY, NZ)
    lane2 = lax.broadcasted_iota(jnp.int32, (OUT2, NZ), 1)

    def compute(c):
        def pair(q, held):
            acc, above = held
            r0 = c * R + 2 * q
            cols = []
            for a in range(2):
                xf = gflat[pl.ds(r0 + a, NX * MP, stride=NY), :]
                hi = xf.astype(BF16)
                lo = (xf - hi.astype(F32)).astype(BF16)
                cols.append(jnp.concatenate([hi, lo, hi], 0))
            v = dot(w[...], jnp.concatenate(cols, 1))
            for a in range(2):
                r = r0 + a
                sums = [None] * 6
                for k in range(KT):
                    vk = v[k * OUT2:(k + 1) * OUT2, a * NZ:(a + 1) * NZ]
                    for d, (kind, at) in enumerate(((0, 0), (1, 0), (2, 0), (2, 1), (3, 0), (4, 0))):
                        term = cf[kind, k, pl.ds(r + at, 1), :] * vk
                        sums[d] = term if sums[d] is None else sums[d] + term
                xlo, xhi, ylo, yhi, zlo, zhi_ = sums
                tlo_flat[pl.ds(r, OUT2, stride=NY), :] = xlo
                thi_flat[pl.ds(r, OUT2, stride=NY), :] = xhi
                pflat[pl.ds(r + R - 1, OUT2, stride=PR), :] = acc - ylo
                acc = ((xlo + xhi) + (ylo + yhi)) + (zlo + zhi_) - above
                acc = acc - jnp.where(lane2 == 0, 0.0, pltpu.roll(zhi_, 1, 1))
                acc = acc - jnp.where(lane2 == NZ - 1, 0.0, pltpu.roll(zlo, NZ - 1, 1))
                above = yhi
            return acc, above

        acc, above = lax.fori_loop(0, R // 2, pair, (carry[0], carry[1]))
        carry[0] = acc
        carry[1] = above

    def send_halos(c):
        when(up, lambda: halo_up(1, c).start())
        when(down, lambda: halo_down(1, c).start())
        when(up & jnp.logical_not(seam_up), lambda: halo_up(0, c).start())
        when(down & jnp.logical_not(seam_down), lambda: halo_down(0, c).start())
        when(seam_up, lambda: aside_up(0, c).start())
        when(seam_down, lambda: aside_down(0, c).start())

    def join(o, c):
        when(down, lambda: halo_up(o, c).wait_recv())
        when(up, lambda: halo_down(o, c).wait_recv())
        here = part[o, 0:MD, rows(c, R)]
        part[o, 0:MD, rows(c, R)] = here - (hlo[o, 0:MD, rows(c)] + hhi[o, 0:MD, rows(c)])

    def step(t, _):
        @pl.when(t + AHEAD < NC)
        def _():
            gather(t + AHEAD, 0)

        @pl.when(t < NC)
        def _():
            for i in range(3):
                got(i, t).wait_recv()

        @pl.when((t >= BACK) & (t < NC + BACK) & relay)
        def _():
            c = t - BACK
            aside_up(0, c).wait_recv()
            when(core == 1, lambda: relay_on_up(0, c).start())
            when(core == 0, lambda: relay_on_down(0, c).start())

        @pl.when(t < NC)
        def _():
            compute(t)
            send_halos(t)

            @pl.when(t == NC - 1)
            def _():
                pflat[pl.ds(NY - 1 + R, OUT2, stride=PR), :] = carry[0]

        @pl.when((t >= lag) & (t < NC + lag))
        def _():
            c = t - lag
            join(1, c)
            across(c).start()

        @pl.when((t >= lag + LATE) & (t < NC + lag + LATE))
        def _():
            c = t - lag - LATE
            join(0, c)
            keep(c).start()

        return 0

    lax.fori_loop(0, NC + LAG + SEAM + LATE, step, 0)

    def drain(c, _):
        for i in range(3):
            own(i, c).wait_send()
        for o in range(2):
            when(up, lambda: halo_up(o, c).wait_send())
            when(down, lambda: halo_down(o, c).wait_send())
        keep(c).wait()
        when(relay, lambda: relay_on_up(0, c).wait_send())
        across(c).wait_send()
        across(c).wait_recv()
        return 0

    for k in range(KT):
        when(up, lambda: field_up(k).wait_send())
        when(down, lambda: field_down(k).wait_send())
        if k % 2 == 0:
            when(relay, lambda: field_relay_up(k).wait_send())

    lax.fori_loop(0, NC, drain, 0)


def local(mode_coeffs, mean_perm, kl_fields, couplings):
    dma = pltpu.SemaphoreType.DMA
    hbm = pl.BlockSpec(memory_space=pl.ANY)
    vmem = pltpu.VMEM
    plane = jax.ShapeDtypeStruct((MD, NY, NZ), F32)
    own, other = pl.pallas_call(
        kernel,
        out_shape=(plane, plane),
        in_specs=[hbm] * 4,
        out_specs=(hbm, hbm),
        scratch_shapes=[
            vmem((NX, MP, NY, NZ), F32),
            vmem((KT, NY, NZ), F32),
            vmem((KT, NY, NZ), F32),
            vmem((KT, NY, NZ), F32),
            vmem((KT, NY, NZ), F32),
            vmem((KT - 1, NY, NY), F32),
            vmem((5, KT, 128, NZ), F32),
            vmem((KT * OUT2, KD), BF16),
            vmem((2, MP, PR, NZ), F32),
            vmem((2, MP, NY, NZ), F32),
            vmem((2, MP, NY, NZ), F32),
            vmem((2, MP, NY, NZ), F32),
            vmem((2, MP, NY, NZ), F32),
            vmem((2, MP, NY, NZ), F32),
            vmem((2, OUT2, NZ), F32),
            dma((4,)), dma((NC,)),
            dma((3, NC)), dma((3, NC)),
            dma((4, NC)), dma((4, NC)),
            dma((2, NC)), dma((2, NC)),
            dma((NC,)), dma((NC,)),
            dma((2, KT)), dma((2, KT)),
            dma((KT,)), dma((KT,)),
        ],
        compiler_params=pltpu.CompilerParams(
            collective_id=0, has_side_effects=True, vmem_limit_bytes=56 * 1024 * 1024
        ),
    )(mode_coeffs.reshape(MD, NY, NZ), mean_perm.reshape(NY, NZ), kl_fields.reshape(KT - 1, NY, NZ), couplings)
    return (own + other).reshape(MD, 1, NY, NZ)


def solution(mesh):
    in_specs = (
        P("modes", "space", None, None),
        P("space", None, None),
        P(None, "space", None, None),
        P(),
    )
    out_specs = P("modes", "space", None, None)
    return jax.shard_map(local, mesh=mesh, in_specs=in_specs, out_specs=out_specs, check_vma=False)
```
